32 devices in a mesh: groups: 2 (over y), seq: 8 (over z, x), tensor: 2 (over core).
Axes of the slice: x: 2, y: 2, z: 4, core: 2. Of those that a mesh axis runs over, the one named last changes fastest.
Arguments:
- queries: bfloat16 [2048, 1536], P(('groups', 'seq'), 'tensor'), parts along dimension 0, may hold values from -64 to 64
- keys: bfloat16 [2048, 1536], P(('groups', 'seq'), 'tensor'), parts along dimension 0, may hold values from -6 to 6
- values: bfloat16 [2048, 1536], P(('groups', 'seq'), 'tensor'), parts along dimension 0, may hold values from -6 to 6
- text_keys: bfloat16 [64, 1536], P(('groups', 'seq'), 'tensor'), parts along dimension 0, may hold values from -6 to 6
- text_values: bfloat16 [64, 1536], P(('groups', 'seq'), 'tensor'), parts along dimension 0, may hold values from -6 to 6
- conv_weight: bfloat16 [4, 1536], P(None, 'tensor'), may hold values from -3 to 3
- out_weight: bfloat16 [1536, 1536], P('tensor'), may hold values from -0.15625 to 0.15625
- image_hidden: bfloat16 [2048, 1536], P(('groups', 'seq')), parts along dimension 0, may hold values from -6 to 6
- gate: bfloat16 [3072], P('groups'), parts along dimension 0, may hold values from -8 to 8
Outputs:
- mixed: bfloat16 [2048, 1536], P(('groups', 'seq')), parts along dimension 0
The draws below stay inside these ranges and needn't reach their ends.
There are 2 independent parts, one for each index of `groups`. The reference program is written for one: setup_inputs(seed, part) draws one part's arguments, and reference() takes and returns one part's arrays. A program takes and returns all parts, laid end to end along the dimension named above; an argument that names none is the same for every part. Nothing has to cross between parts.
All inputs are finite; a program needn't handle non-finite values.
Results may differ from the reference program's by a relative error of at most 0.011.
Values may be sent and summed in bfloat16 or wider, within the bound.
A program may use at most 64 MiB of HBM per device.

```python
import math
import jax
import jax.numpy as jnp
from jax import lax

HEADS = 12
HEAD_DIM = 128
DOUT = 1536
ROW_TOKENS = 64
IMG_ROWS = 16
TOKENS = 1024
TEXT = 32


def draw_text_keys(key, part):
    features = HEADS * HEAD_DIM
    drawn = jnp.clip(jax.random.normal(jax.random.fold_in(key, 5), (TEXT, features), jnp.float32), -6.0, 6.0)
    return drawn.astype(jnp.bfloat16)


def draw_queries(key, part):
    features = HEADS * HEAD_DIM
    drawn = 2.5 * jnp.clip(jax.random.normal(jax.random.fold_in(key, 7), (TOKENS, features), jnp.float32), -6.0, 6.0)
    return drawn.astype(jnp.bfloat16)


def shard_levels(own_key, dims, cuts, smallest, high):
    factor_of = 1.0
    for axis_at, blocks in cuts:
        draws = jax.random.uniform(jax.random.fold_in(jax.random.fold_in(own_key, 6), axis_at), (blocks,), jnp.float32, smallest / len(cuts), high / len(cuts))
        factor_of = factor_of * jnp.repeat(jnp.exp(draws), dims[axis_at] // blocks).reshape((-1,) + (1,) * (len(dims) - 1 - axis_at))
    return factor_of


def scatter_about(rng, extent, width, reach, split=(), kind=jnp.bfloat16):
    gain = shard_levels(rng, extent, split, -0.22, 0.18) if split else 1.0
    values = jax.random.normal(rng, extent, jnp.float32) * width * gain
    return jnp.minimum(jnp.maximum(values, -reach), reach).astype(kind)


def setup_inputs(seed: int = 0, part: int = 0) -> dict:
    key_list = jax.random.split(jax.random.key(seed), 10)
    part_keys = jax.random.split(jax.random.fold_in(key_list[9], part), 10)
    queries = draw_queries(jax.random.fold_in(jax.random.fold_in(key_list[9], part), 71), part)
    keys = scatter_about(part_keys[1], (TOKENS, HEADS * HEAD_DIM), 1.0, 6.0, ((0, 8), (1, 2)))
    values = scatter_about(part_keys[2], (TOKENS, HEADS * HEAD_DIM), 1.0, 6.0, ((0, 8), (1, 2)))
    text_keys = draw_text_keys(jax.random.fold_in(jax.random.fold_in(key_list[9], part), 71), part)
    text_values = scatter_about(part_keys[4], (TEXT, HEADS * HEAD_DIM), 1.0, 6.0, ((0, 8), (1, 2)))
    conv_weight = scatter_about(key_list[5], (4, HEADS * HEAD_DIM), 0.5, 3.0, ((1, 2),))
    out_weight = scatter_about(key_list[6], (HEADS * HEAD_DIM, DOUT), (HEADS * HEAD_DIM) ** -0.5, 0.15625, ((0, 2),))
    image_hidden = scatter_about(part_keys[7], (TOKENS, DOUT), 1.0, 6.0, ((0, 8),))
    gate = scatter_about(part_keys[8], (DOUT,), 2.0, 8.0)
    return dict(queries=queries, keys=keys, values=values, text_keys=text_keys, text_values=text_values, conv_weight=conv_weight, out_weight=out_weight, image_hidden=image_hidden, gate=gate)


def rope_angles(row_pos, col_pos, head_dim):
    lead_dims = head_dim // 8
    group_dims = head_dim * 7 // 16
    frequency = 10000.0 ** (-(2.0 * jnp.arange(group_dims // 2, dtype=jnp.float32)) / group_dims)
    zero_angles = jnp.zeros((row_pos.shape[0], lead_dims // 2), jnp.float32)
    return jnp.concatenate([zero_angles, row_pos[:, None] * frequency[None, :], col_pos[:, None] * frequency[None, :]], axis=1)

def apply_rope(field, angles):
    paired = field.reshape(field.shape[0], field.shape[1], field.shape[2] // 2, 2)
    even_part = paired[..., 0]
    odd_part = paired[..., 1]
    cos_part = jnp.cos(angles)[:, None, :]
    sin_part = jnp.sin(angles)[:, None, :]
    turned = jnp.stack([even_part * cos_part - odd_part * sin_part, even_part * sin_part + odd_part * cos_part], axis=-1)
    return turned.reshape(field.shape)

def reference(queries, keys, values, text_keys, text_values, conv_weight, out_weight, image_hidden, gate):
    features = HEADS * HEAD_DIM
    taps = conv_weight.astype(jnp.float32).reshape(2, 2, features)

    def compress(field):
        grid_cells = field.astype(jnp.float32).reshape(IMG_ROWS // 2, 2, ROW_TOKENS // 2, 2, features)
        return (grid_cells[:, 0, :, 0] * taps[0, 0] + grid_cells[:, 0, :, 1] * taps[0, 1] + grid_cells[:, 1, :, 0] * taps[1, 0] + grid_cells[:, 1, :, 1] * taps[1, 1]).reshape(-1, features)
    token_ids = jnp.arange(TOKENS, dtype=jnp.int32)
    angles_query = rope_angles((token_ids // ROW_TOKENS).astype(jnp.float32), (token_ids % ROW_TOKENS).astype(jnp.float32), HEAD_DIM)
    queries_rot = apply_rope(queries.astype(jnp.float32).reshape(TOKENS, HEADS, HEAD_DIM), angles_query).astype(jnp.bfloat16)
    half_width = ROW_TOKENS // 2
    patch_ids = jnp.arange(TOKENS // 4, dtype=jnp.int32)
    angles_key = rope_angles(2.0 * (patch_ids // half_width).astype(jnp.float32) + 0.5, 2.0 * (patch_ids % half_width).astype(jnp.float32) + 0.5, HEAD_DIM)
    short_keys = apply_rope(compress(keys).reshape(TOKENS // 4, HEADS, HEAD_DIM), angles_key).astype(jnp.bfloat16)
    short_values = compress(values).astype(jnp.bfloat16).reshape(TOKENS // 4, HEADS, HEAD_DIM)
    all_keys = jnp.concatenate([short_keys, text_keys.reshape(TEXT, HEADS, HEAD_DIM)], axis=0).astype(jnp.float32)
    all_values = jnp.concatenate([short_values, text_values.reshape(TEXT, HEADS, HEAD_DIM)], axis=0).astype(jnp.float32)
    inv_root = 1.0 / math.sqrt(HEAD_DIM)

    def attend(query_rows):
        scores = jnp.einsum('qhd,khd->hqk', query_rows.astype(jnp.float32), all_keys) * inv_root
        weights = jnp.exp(scores - lax.optimization_barrier(jnp.max(scores, axis=-1, keepdims=True))).astype(jnp.bfloat16)
        totals = lax.optimization_barrier(jnp.sum(weights.astype(jnp.float32), axis=-1))
        summed = jnp.einsum('hqk,khd->qhd', weights.astype(jnp.float32), all_values)
        return (summed / totals.T[:, :, None]).astype(jnp.bfloat16)
    query_block = 512 if TOKENS % 512 == 0 else TOKENS
    attended = lax.map(attend, queries_rot.reshape(TOKENS // query_block, query_block, HEADS, HEAD_DIM)).reshape(TOKENS, features)
    projected = jnp.dot(attended, out_weight, preferred_element_type=jnp.float32)
    return (image_hidden.astype(jnp.float32) + gate.astype(jnp.float32)[None, :] * projected).astype(jnp.bfloat16)
```

```python
import functools
import math

import jax
import jax.numpy as jnp
import numpy as np
from jax import lax
from jax.experimental import pallas as pl
from jax.experimental.pallas import tpu as pltpu
from jax.sharding import PartitionSpec as P

HEAD_DIM = 128
MESH = pl.DeviceIdType.MESH


def position_tables(places, row_width):
    lead = HEAD_DIM // 8
    group = HEAD_DIM * 7 // 16
    frequency = np.power(
        np.float32(10000.0), -(2.0 * np.arange(group // 2, dtype=np.float32)) / np.float32(group)
    ).astype(np.float32)
    pair_frequency = np.repeat(frequency, 2)
    sign = np.where(np.arange(group) % 2 == 0, -1.0, 1.0)

    def turned(positions):
        angles = (np.asarray(positions, np.float32)[:, None] * pair_frequency[None, :]).astype(np.float64)
        return np.cos(angles), np.sin(angles) * sign

    def row_part(positions):
        cos_part, sin_part = turned(positions)
        count = len(positions)
        full_cos = np.zeros((count, HEAD_DIM))
        full_sin = np.zeros((count, HEAD_DIM))
        full_cos[:, :lead] = 1.0
        full_cos[:, lead : lead + group] = cos_part
        full_sin[:, lead : lead + group] = sin_part
        return full_cos, full_sin

    def col_part(positions):
        cos_part, sin_part = turned(positions)
        count = len(positions)
        full_cos = np.zeros((count, HEAD_DIM))
        full_sin = np.zeros((count, HEAD_DIM))
        full_cos[:, lead + group :] = cos_part
        full_sin[:, lead + group :] = sin_part
        return full_cos, full_sin

    place = np.arange(places, dtype=np.float32)
    rows = np.zeros((places, 8, HEAD_DIM))
    rows[:, 0], rows[:, 2] = row_part(2.0 * place)
    rows[:, 1], rows[:, 3] = row_part(2.0 * place + 1.0)
    rows[:, 4], rows[:, 5] = row_part(2.0 * place + 0.5)
    cos_q, sin_q = col_part(np.arange(row_width))
    cos_k, sin_k = col_part(2.0 * np.arange(row_width // 2) + 0.5)
    cols = np.concatenate([cos_q, sin_q, cos_k, sin_k], axis=0)
    return rows.astype(np.float32), cols.astype(np.float32)


def fused(
    places, inner, queries, keys, values, text_keys, text_values, conv_weight, out_weight, image_hidden,
    gate, row_table, col_table, mixed, key_buf, value_buf, text_buf, text_all, query_in, key_in, value_in,
    weight_buf, hidden_buf, query_rot, attended, own_part, peer_part, load_sem, key_send, key_recv,
    value_send, value_recv, text_send, text_recv, part_send, part_recv,
):
    tokens, features = query_in.shape
    heads = features // HEAD_DIM
    row_width = tokens // 2
    patches = row_width // 2
    text_rows = text_buf.shape[2]
    outer = places // inner
    parts = own_part.shape[0]
    part_width = own_part.shape[2]
    me = lax.axis_index("seq")
    core = lax.axis_index("tensor")
    my_outer = me // inner
    my_inner = lax.rem(me, inner)

    loads = [
        pltpu.make_async_copy(keys, key_in, load_sem.at[0]),
        pltpu.make_async_copy(values, value_in, load_sem.at[1]),
        pltpu.make_async_copy(text_keys, text_buf.at[me, 0], load_sem.at[2]),
        pltpu.make_async_copy(text_values, text_buf.at[me, 1], load_sem.at[3]),
        pltpu.make_async_copy(queries, query_in, load_sem.at[4]),
        pltpu.make_async_copy(out_weight, weight_buf, load_sem.at[5]),
        pltpu.make_async_copy(image_hidden, hidden_buf, load_sem.at[6]),
    ]
    for load in loads:
        load.start()

    barrier = pltpu.get_barrier_semaphore()
    for step in range(1, places):
        pl.semaphore_signal(
            barrier, inc=1, device_id={"seq": lax.rem(me + step, places)}, device_id_type=MESH
        )
    pl.semaphore_signal(barrier, inc=1, device_id={"tensor": 1 - core}, device_id_type=MESH)

    row_of = lax.broadcasted_iota(jnp.int32, (tokens, tokens), 0)
    token_of = lax.broadcasted_iota(jnp.int32, (tokens, tokens), 1)
    tap_of = row_of // patches
    wanted = (tap_of // 2) * row_width + 2 * (row_of % patches) + tap_of % 2
    pick = (token_of == wanted).astype(jnp.bfloat16)
    taps = conv_weight[...].astype(jnp.float32)

    def compress(field):
        picked = jnp.dot(pick, field, preferred_element_type=jnp.float32)
        total = picked[:patches] * taps[0:1]
        for tap in range(1, 4):
            total = total + picked[tap * patches : (tap + 1) * patches] * taps[tap : tap + 1]
        return total

    my_rows = row_table[me]
    cos_k = my_rows[4:5] + col_table[2 * row_width : 2 * row_width + patches]
    sin_k = my_rows[5:6] + col_table[2 * row_width + patches : 2 * row_width + 2 * patches]
    even = lax.broadcasted_iota(jnp.int32, (patches, HEAD_DIM), 1) % 2 == 0
    loads[0].wait()
    short_raw = compress(key_in[...])
    for head in range(heads):
        lanes = slice(head * HEAD_DIM, (head + 1) * HEAD_DIM)
        raw = short_raw[:, lanes]
        swapped = jnp.where(even, pltpu.roll(raw, HEAD_DIM - 1, 1), pltpu.roll(raw, 1, 1))
        key_buf[me, :, lanes] = (raw * cos_k + swapped * sin_k).astype(jnp.bfloat16)
    loads[1].wait()
    value_buf[me] = compress(value_in[...]).astype(jnp.bfloat16)
    loads[2].wait()
    loads[3].wait()

    pl.semaphore_wait(barrier, places)

    sends = []

    def send(buf, slot, send_sem, recv_sem, at, target):
        copy = pltpu.make_async_remote_copy(
            src_ref=buf.at[slot],
            dst_ref=buf.at[slot],
            send_sem=send_sem.at[at],
            recv_sem=recv_sem.at[slot],
            device_id={"seq": target},
            device_id_type=MESH,
        )
        copy.start()
        sends.append(copy)

    def arrive(buf, slot, send_sem, recv_sem):
        pltpu.make_async_remote_copy(
            src_ref=buf.at[slot],
            dst_ref=buf.at[slot],
            send_sem=send_sem.at[0],
            recv_sem=recv_sem.at[slot],
            device_id={"seq": me},
            device_id_type=MESH,
        ).wait_recv()

    outer_peers = [lax.rem(my_outer + step, outer) for step in range(1, outer)]
    inner_peers = [lax.rem(my_inner + step, inner) for step in range(1, inner)]

    def send_own(buf, send_sem, recv_sem):
        at = 0
        for peer in outer_peers:
            send(buf, me, send_sem, recv_sem, at, peer * inner + my_inner)
            at += 1
        for peer in inner_peers:
            send(buf, me, send_sem, recv_sem, at, my_outer * inner + peer)
            at += 1

    def forward(buf, send_sem, recv_sem):
        at = outer - 1 + inner - 1
        for step in range(outer - 1, 0, -1):
            source = lax.rem(my_outer + step, outer) * inner + my_inner
            arrive(buf, source, send_sem, recv_sem)
            for peer in inner_peers:
                send(buf, source, send_sem, recv_sem, at, my_outer * inner + peer)
                at += 1

    def collect(buf, send_sem, recv_sem):
        for peer in inner_peers:
            for step in range(outer):
                source = lax.rem(my_outer + outer - step, outer) * inner + peer
                arrive(buf, source, send_sem, recv_sem)

    send_own(key_buf, key_send, key_recv)
    for step in range(1, places):
        send(text_buf, me, text_send, text_recv, step, lax.rem(me + step, places))
    send_own(value_buf, value_send, value_recv)

    loads[4].wait()
    first = lax.broadcasted_iota(jnp.int32, (HEAD_DIM, HEAD_DIM), 0)
    second = lax.broadcasted_iota(jnp.int32, (HEAD_DIM, HEAD_DIM), 1)
    swap = (first == second + 1 - 2 * (second % 2)).astype(jnp.bfloat16)
    col_cos = col_table[:row_width]
    col_sin = col_table[row_width : 2 * row_width]
    for row in range(2):
        cos_q = my_rows[row : row + 1] + col_cos
        sin_q = my_rows[2 + row : 3 + row] + col_sin
        rows = slice(row * row_width, (row + 1) * row_width)
        for head in range(heads):
            lanes = slice(head * HEAD_DIM, (head + 1) * HEAD_DIM)
            plain = query_in[rows, lanes]
            crossed = jnp.dot(plain, swap, preferred_element_type=jnp.float32)
            query_rot[rows, lanes] = (plain.astype(jnp.float32) * cos_q + crossed * sin_q).astype(jnp.bfloat16)

    forward(key_buf, key_send, key_recv)

    for step in range(1, places):
        arrive(text_buf, lax.rem(me + step, places), text_send, text_recv)
    for kind in range(2):
        for place in range(places):
            text_all[kind, place * text_rows : (place + 1) * text_rows, :] = text_buf[place, kind].astype(
                jnp.float32
            )

    collect(key_buf, key_send, key_recv)
    forward(value_buf, value_send, value_recv)

    scale = 1.0 / math.sqrt(HEAD_DIM)
    across = (((1,), (1,)), ((), ()))
    held = []
    for head in range(heads):
        lanes = slice(head * HEAD_DIM, (head + 1) * HEAD_DIM)
        turned = query_rot[:, lanes]
        short = key_buf[:, :, lanes].reshape(places * patches, HEAD_DIM)
        text = text_all[0, :, lanes].astype(jnp.bfloat16)
        short_scores = lax.dot_general(turned, short, across, preferred_element_type=jnp.float32)
        text_scores = lax.dot_general(turned, text, across, preferred_element_type=jnp.float32)
        top = jnp.maximum(
            jnp.max(short_scores, axis=-1, keepdims=True), jnp.max(text_scores, axis=-1, keepdims=True)
        )
        short_weights = jnp.exp((short_scores - top) * scale).astype(jnp.bfloat16)
        text_weights = jnp.exp((text_scores - top) * scale).astype(jnp.bfloat16)
        total = jnp.sum(short_weights.astype(jnp.float32), axis=-1, keepdims=True) + jnp.sum(
            text_weights.astype(jnp.float32), axis=-1, keepdims=True
        )
        held.append((short_weights, text_weights, 1.0 / total))

    collect(value_buf, value_send, value_recv)
    for head in range(heads):
        lanes = slice(head * HEAD_DIM, (head + 1) * HEAD_DIM)
        short_weights, text_weights, inverse = held[head]
        short = value_buf[:, :, lanes].reshape(places * patches, HEAD_DIM)
        text = text_all[1, :, lanes].astype(jnp.bfloat16)
        summed = jnp.dot(short_weights, short, preferred_element_type=jnp.float32) + jnp.dot(
            text_weights, text, preferred_element_type=jnp.float32
        )
        attended[:, lanes] = (summed * inverse).astype(jnp.bfloat16)

    loads[5].wait()
    exchanges = []
    for part in range(parts):
        lanes = slice(part * part_width, (part + 1) * part_width)
        own_part[part] = jnp.dot(
            attended[...], weight_buf[:, lanes], preferred_element_type=jnp.float32
        ).astype(jnp.bfloat16)
        exchange = pltpu.make_async_remote_copy(
            src_ref=own_part.at[part],
            dst_ref=peer_part.at[part],
            send_sem=part_send.at[part],
            recv_sem=part_recv.at[part],
            device_id={"tensor": 1 - core},
            device_id_type=MESH,
        )
        exchange.start()
        exchanges.append(exchange)
    loads[6].wait()
    for part in range(parts):
        lanes = slice(part * part_width, (part + 1) * part_width)
        exchanges[part].wait_recv()
        projected = own_part[part].astype(jnp.float32) + peer_part[part].astype(jnp.float32)
        mixed[:, lanes] = (
            hidden_buf[:, lanes].astype(jnp.float32) + gate[:, lanes].astype(jnp.float32) * projected
        ).astype(jnp.bfloat16)
    for copy in sends + exchanges:
        copy.wait_send()


def local(
    places, queries, keys, values, text_keys, text_values, conv_weight, out_weight, image_hidden, gate
):
    tokens, features = queries.shape
    width = out_weight.shape[1]
    patches = tokens // 4
    text_rows = text_keys.shape[0]
    inner = 1 << ((places.bit_length() - 1) // 2)
    if places % inner:
        inner = 1
    row_table, col_table = position_tables(places, tokens // 2)
    parts = 3
    bf16, f32 = jnp.bfloat16, jnp.float32
    hbm = pl.BlockSpec(memory_space=pl.ANY)
    vmem = pl.BlockSpec(memory_space=pltpu.VMEM)
    sems = pltpu.SemaphoreType.DMA
    return pl.pallas_call(
        functools.partial(fused, places, inner),
        out_shape=jax.ShapeDtypeStruct((tokens, width), bf16),
        in_specs=[hbm, hbm, hbm, hbm, hbm, vmem, hbm, hbm, vmem, vmem, vmem],
        out_specs=vmem,
        scratch_shapes=[
            pltpu.VMEM((places, patches, features), bf16),
            pltpu.VMEM((places, patches, features), bf16),
            pltpu.VMEM((places, 2, text_rows, features), bf16),
            pltpu.VMEM((2, places * text_rows, features), f32),
            pltpu.VMEM((tokens, features), bf16),
            pltpu.VMEM((tokens, features), bf16),
            pltpu.VMEM((tokens, features), bf16),
            pltpu.VMEM((features, width), bf16),
            pltpu.VMEM((tokens, width), bf16),
            pltpu.VMEM((tokens, features), bf16),
            pltpu.VMEM((tokens, features), bf16),
            pltpu.VMEM((parts, tokens, width // parts), bf16),
            pltpu.VMEM((parts, tokens, width // parts), bf16),
            sems((7,)),
            sems((places,)),
            sems((places,)),
            sems((places,)),
            sems((places,)),
            sems((places,)),
            sems((places,)),
            sems((parts,)),
            sems((parts,)),
        ],
        compiler_params=pltpu.CompilerParams(collective_id=0, has_side_effects=True),
        name="joint_attention",
    )(
        queries, keys, values, text_keys, text_values, conv_weight, out_weight, image_hidden,
        gate.reshape(1, width), jnp.asarray(row_table), jnp.asarray(col_table),
    )


def solution(mesh):
    placed = (
        P(("groups", "seq"), "tensor"),
        P(("groups", "seq"), "tensor"),
        P(("groups", "seq"), "tensor"),
        P(("groups", "seq"), "tensor"),
        P(("groups", "seq"), "tensor"),
        P(None, "tensor"),
        P("tensor", None),
        P(("groups", "seq"), None),
        P("groups"),
    )
    return jax.shard_map(
        functools.partial(local, mesh.shape["seq"]),
        mesh=mesh,
        in_specs=placed,
        out_specs=P(("groups", "seq"), None),
        check_vma=False,
    )
```

```python
import functools
import math

import jax
import jax.numpy as jnp
import numpy as np
from jax import lax
from jax.experimental import pallas as pl
from jax.experimental.pallas import tpu as pltpu
from jax.sharding import PartitionSpec as P

HEAD_DIM = 128
MESH = pl.DeviceIdType.MESH


def position_tables(places, row_width):
    lead = HEAD_DIM // 8
    group = HEAD_DIM * 7 // 16
    frequency = np.power(
        np.float32(10000.0), -(2.0 * np.arange(group // 2, dtype=np.float32)) / np.float32(group)
    ).astype(np.float32)
    pair_frequency = np.repeat(frequency, 2)
    sign = np.where(np.arange(group) % 2 == 0, -1.0, 1.0)

    def turned(positions):
        angles = (np.asarray(positions, np.float32)[:, None] * pair_frequency[None, :]).astype(np.float64)
        return np.cos(angles), np.sin(angles) * sign

    def row_part(positions):
        cos_part, sin_part = turned(positions)
        count = len(positions)
        full_cos = np.zeros((count, HEAD_DIM))
        full_sin = np.zeros((count, HEAD_DIM))
        full_cos[:, :lead] = 1.0
        full_cos[:, lead : lead + group] = cos_part
        full_sin[:, lead : lead + group] = sin_part
        return full_cos, full_sin

    def col_part(positions):
        cos_part, sin_part = turned(positions)
        count = len(positions)
        full_cos = np.zeros((count, HEAD_DIM))
        full_sin = np.zeros((count, HEAD_DIM))
        full_cos[:, lead + group :] = cos_part
        full_sin[:, lead + group :] = sin_part
        return full_cos, full_sin

    place = np.arange(places, dtype=np.float32)
    rows = np.zeros((places, 8, HEAD_DIM))
    rows[:, 0], rows[:, 2] = row_part(2.0 * place)
    rows[:, 1], rows[:, 3] = row_part(2.0 * place + 1.0)
    rows[:, 4], rows[:, 5] = row_part(2.0 * place + 0.5)
    cos_q, sin_q = col_part(np.arange(row_width))
    cos_k, sin_k = col_part(2.0 * np.arange(row_width // 2) + 0.5)
    cols = np.concatenate([cos_q, sin_q, cos_k, sin_k], axis=0)
    return rows.astype(np.float32), cols.astype(np.float32)


def fused(
    places, inner, queries, keys, values, text_keys, text_values, conv_weight, out_weight, image_hidden,
    gate, row_table, col_table, mixed, key_buf, value_buf, text_buf, text_all, query_in, key_in, value_in,
    weight_buf, hidden_buf, taps_buf, gate_buf, rows_buf, cols_buf, query_rot, attended, own_part, peer_part,
    load_sem, key_send, key_recv, value_send, value_recv, text_send, text_recv, part_send, part_recv,
):
    tokens, features = query_in.shape
    heads = features // HEAD_DIM
    row_width = tokens // 2
    patches = row_width // 2
    text_rows = text_keys.shape[0]
    outer = places // inner
    parts = own_part.shape[0]
    part_width = own_part.shape[2]
    me = lax.axis_index("seq")
    core = lax.axis_index("tensor")
    along = me // inner
    across = lax.rem(me, inner)
    inner_peers = [lax.rem(across + step, inner) for step in range(1, inner)]

    def at_place(outer_at, inner_at):
        return {"seq": outer_at * inner + inner_at}

    def inside(outer_at):
        return jnp.logical_and(outer_at >= 0, outer_at < outer)

    barrier = pltpu.get_barrier_semaphore()
    near = [move for move in (1, -1, 2, -2) if abs(move) < outer]
    for move in near:

        @pl.when(inside(along + move))
        def _():
            pl.semaphore_signal(
                barrier, inc=1, device_id=at_place(along + move, across), device_id_type=MESH
            )

    for peer in inner_peers:
        pl.semaphore_signal(barrier, inc=1, device_id=at_place(along, peer), device_id_type=MESH)
    pl.semaphore_signal(barrier, inc=1, device_id={"tensor": 1 - core}, device_id_type=MESH)

    loads = [
        pltpu.make_async_copy(keys, key_in, load_sem.at[0]),
        pltpu.make_async_copy(conv_weight, taps_buf, load_sem.at[1]),
        pltpu.make_async_copy(row_table.at[me], rows_buf, load_sem.at[2]),
        pltpu.make_async_copy(col_table, cols_buf, load_sem.at[3]),
        pltpu.make_async_copy(values, value_in, load_sem.at[4]),
        pltpu.make_async_copy(text_keys, text_buf.at[across, along, 0], load_sem.at[5]),
        pltpu.make_async_copy(text_values, text_buf.at[across, along, 1], load_sem.at[6]),
        pltpu.make_async_copy(queries, query_in, load_sem.at[7]),
        pltpu.make_async_copy(out_weight, weight_buf, load_sem.at[8]),
        pltpu.make_async_copy(image_hidden, hidden_buf, load_sem.at[9]),
        pltpu.make_async_copy(gate, gate_buf, load_sem.at[10]),
    ]
    for load in loads:
        load.start()

    row_of = lax.broadcasted_iota(jnp.int32, (tokens, tokens), 0)
    token_of = lax.broadcasted_iota(jnp.int32, (tokens, tokens), 1)
    tap_of = row_of // patches
    wanted = (tap_of // 2) * row_width + 2 * (row_of % patches) + tap_of % 2
    pick = (token_of == wanted).astype(jnp.bfloat16)
    for load in loads[:4]:
        load.wait()
    taps = taps_buf[...].astype(jnp.float32)

    def compress(field):
        picked = jnp.dot(pick, field, preferred_element_type=jnp.float32)
        total = picked[:patches] * taps[0:1]
        for tap in range(1, 4):
            total = total + picked[tap * patches : (tap + 1) * patches] * taps[tap : tap + 1]
        return total

    my_rows = rows_buf[...]
    cos_k = my_rows[4:5] + cols_buf[2 * row_width : 2 * row_width + patches]
    sin_k = my_rows[5:6] + cols_buf[2 * row_width + patches : 2 * row_width + 2 * patches]
    even = lax.broadcasted_iota(jnp.int32, (patches, HEAD_DIM), 1) % 2 == 0
    short_raw = compress(key_in[...])
    for head in range(heads):
        lanes = slice(head * HEAD_DIM, (head + 1) * HEAD_DIM)
        raw = short_raw[:, lanes]
        swapped = jnp.where(even, pltpu.roll(raw, HEAD_DIM - 1, 1), pltpu.roll(raw, 1, 1))
        key_buf[across, along, :, lanes] = (raw * cos_k + swapped * sin_k).astype(jnp.bfloat16)
    loads[4].wait()
    value_buf[across, along] = compress(value_in[...]).astype(jnp.bfloat16)
    loads[5].wait()
    loads[6].wait()

    pl.semaphore_wait(barrier, inner + sum(inside(along + move).astype(jnp.int32) for move in near))

    closing = []

    def copy_of(buf, slot, send_sem, recv_sem, number, target):
        return pltpu.make_async_remote_copy(
            src_ref=buf.at[slot[0], slot[1]],
            dst_ref=buf.at[slot[0], slot[1]],
            send_sem=send_sem.at[number],
            recv_sem=recv_sem.at[slot[0], slot[1]],
            device_id=target,
            device_id_type=MESH,
        )

    def send(buf, slot, send_sem, recv_sem, number, target, when=None):
        def begin():
            copy_of(buf, slot, send_sem, recv_sem, number, target).start()

        def end():
            copy_of(buf, slot, send_sem, recv_sem, number, target).wait_send()

        if when is None:
            begin()
            closing.append(end)
        else:
            pl.when(when)(begin)
            closing.append(lambda: pl.when(when)(end))

    def send_own(buf, send_sem, recv_sem):
        for number, move in enumerate(near):
            send(
                buf, (across, along), send_sem, recv_sem, number, at_place(along + move, across),
                inside(along + move),
            )
        for number, peer in enumerate(inner_peers):
            send(buf, (across, along), send_sem, recv_sem, 4 + number, at_place(along, peer))

    def pass_on(buf, send_sem, recv_sem):
        number = 4 + inner - 1
        for distance in range(1, outer):
            for side in (1, -1):
                source = along + side * distance
                slot = (across, jnp.clip(source, 0, outer - 1))
                here = inside(source)

                @pl.when(here)
                def _():
                    copy_of(buf, slot, send_sem, recv_sem, 0, at_place(along, across)).wait_recv()

                further = along - 2 * side
                send(
                    buf, slot, send_sem, recv_sem, number, at_place(further, across),
                    jnp.logical_and(here, inside(further)),
                )
                number += 1
                for peer in inner_peers:
                    send(buf, slot, send_sem, recv_sem, number, at_place(along, peer), here)
                    number += 1

    def collect(buf, send_sem, recv_sem):
        for peer in inner_peers:
            for place in range(outer):
                copy_of(buf, (peer, place), send_sem, recv_sem, 0, at_place(along, across)).wait_recv()

    send_own(key_buf, key_send, key_recv)
    send_own(text_buf, text_send, text_recv)
    send_own(value_buf, value_send, value_recv)

    loads[7].wait()
    first = lax.broadcasted_iota(jnp.int32, (HEAD_DIM, HEAD_DIM), 0)
    second = lax.broadcasted_iota(jnp.int32, (HEAD_DIM, HEAD_DIM), 1)
    swap = (first == second + 1 - 2 * (second % 2)).astype(jnp.bfloat16)
    col_cos = cols_buf[:row_width]
    col_sin = cols_buf[row_width : 2 * row_width]
    for row in range(2):
        cos_q = my_rows[row : row + 1] + col_cos
        sin_q = my_rows[2 + row : 3 + row] + col_sin
        rows = slice(row * row_width, (row + 1) * row_width)
        for head in range(heads):
            lanes = slice(head * HEAD_DIM, (head + 1) * HEAD_DIM)
            plain = query_in[rows, lanes]
            crossed = jnp.dot(plain, swap, preferred_element_type=jnp.float32)
            query_rot[rows, lanes] = (plain.astype(jnp.float32) * cos_q + crossed * sin_q).astype(jnp.bfloat16)

    pass_on(key_buf, key_send, key_recv)
    pass_on(text_buf, text_send, text_recv)
    pass_on(value_buf, value_send, value_recv)

    scale = 1.0 / math.sqrt(HEAD_DIM)
    transposed = (((1,), (1,)), ((), ()))
    lanes_of = [slice(head * HEAD_DIM, (head + 1) * HEAD_DIM) for head in range(heads)]

    def scores_with(keys_of):
        return [
            lax.dot_general(query_rot[:, lanes], keys_of(lanes), transposed, preferred_element_type=jnp.float32)
            for lanes in lanes_of
        ]

    def group_of(buf, at):
        return lambda lanes: buf[at, :, :, lanes].reshape(outer * patches, HEAD_DIM)

    scores = [scores_with(group_of(key_buf, across))]
    collect(text_buf, text_send, text_recv)
    for kind in range(2):
        for place in range(places):
            text_all[kind, place * text_rows : (place + 1) * text_rows, :] = text_buf[
                place // outer, place % outer, kind
            ].astype(jnp.float32)
    scores.append(scores_with(lambda lanes: text_all[0, :, lanes].astype(jnp.bfloat16)))
    collect(key_buf, key_send, key_recv)
    for peer in inner_peers:
        scores.append(scores_with(group_of(key_buf, peer)))

    weights, inverse = [], []
    for head in range(heads):
        top = functools.reduce(
            jnp.maximum, [jnp.max(group[head], axis=-1, keepdims=True) for group in scores]
        )
        weights.append([jnp.exp((group[head] - top) * scale).astype(jnp.bfloat16) for group in scores])
        total = sum(jnp.sum(group.astype(jnp.float32), axis=-1, keepdims=True) for group in weights[head])
        inverse.append(1.0 / total)
    summed = [
        jnp.dot(weights[head][0], group_of(value_buf, across)(lanes), preferred_element_type=jnp.float32)
        + jnp.dot(
            weights[head][1], text_all[1, :, lanes].astype(jnp.bfloat16), preferred_element_type=jnp.float32
        )
        for head, lanes in enumerate(lanes_of)
    ]
    loads[8].wait()
    loads[9].wait()
    loads[10].wait()

    collect(value_buf, value_send, value_recv)
    for head, lanes in enumerate(lanes_of):
        for number, peer in enumerate(inner_peers):
            summed[head] = summed[head] + jnp.dot(
                weights[head][2 + number], group_of(value_buf, peer)(lanes), preferred_element_type=jnp.float32
            )
        attended[:, lanes] = (summed[head] * inverse[head]).astype(jnp.bfloat16)

    exchanges = []
    for part in range(parts):
        lanes = slice(part * part_width, (part + 1) * part_width)
        own_part[part] = jnp.dot(
            attended[...], weight_buf[:, lanes], preferred_element_type=jnp.float32
        ).astype(jnp.bfloat16)
        exchange = pltpu.make_async_remote_copy(
            src_ref=own_part.at[part],
            dst_ref=peer_part.at[part],
            send_sem=part_send.at[part],
            recv_sem=part_recv.at[part],
            device_id={"tensor": 1 - core},
            device_id_type=MESH,
        )
        exchange.start()
        exchanges.append(exchange)
    for end in closing:
        end()
    gates = gate_buf[...].astype(jnp.float32).reshape(1, parts * part_width)
    for part in range(parts):
        lanes = slice(part * part_width, (part + 1) * part_width)
        exchanges[part].wait_recv()
        projected = own_part[part].astype(jnp.float32) + peer_part[part].astype(jnp.float32)
        mixed[:, lanes] = (
            hidden_buf[:, lanes].astype(jnp.float32) + gates[:, lanes] * projected
        ).astype(jnp.bfloat16)
    for exchange in exchanges:
        exchange.wait_send()


def local(
    places, queries, keys, values, text_keys, text_values, conv_weight, out_weight, image_hidden, gate
):
    tokens, features = queries.shape
    width = out_weight.shape[1]
    patches = tokens // 4
    text_rows = text_keys.shape[0]
    inner = 1 << ((places.bit_length() - 1) // 2)
    if places % inner:
        inner = 1
    row_table, col_table = position_tables(places, tokens // 2)
    parts = 3
    bf16, f32 = jnp.bfloat16, jnp.float32
    hbm = pl.BlockSpec(memory_space=pl.ANY)
    vmem = pl.BlockSpec(memory_space=pltpu.VMEM)
    sems = pltpu.SemaphoreType.DMA
    outer = places // inner
    sends = 4 + inner - 1 + 2 * (outer - 1) * inner
    return pl.pallas_call(
        functools.partial(fused, places, inner),
        out_shape=pltpu.VMEM((tokens, width), bf16),
        in_specs=[hbm] * 11,
        out_specs=vmem,
        scratch_shapes=[
            pltpu.VMEM((inner, outer, patches, features), bf16),
            pltpu.VMEM((inner, outer, patches, features), bf16),
            pltpu.VMEM((inner, outer, 2, text_rows, features), bf16),
            pltpu.VMEM((2, places * text_rows, features), f32),
            pltpu.VMEM((tokens, features), bf16),
            pltpu.VMEM((tokens, features), bf16),
            pltpu.VMEM((tokens, features), bf16),
            pltpu.VMEM((features, width), bf16),
            pltpu.VMEM((tokens, width), bf16),
            pltpu.VMEM(conv_weight.shape, bf16),
            pltpu.VMEM(gate.shape, bf16),
            pltpu.VMEM(row_table.shape[1:], f32),
            pltpu.VMEM(col_table.shape, f32),
            pltpu.VMEM((tokens, features), bf16),
            pltpu.VMEM((tokens, features), bf16),
            pltpu.VMEM((parts, tokens, width // parts), bf16),
            pltpu.VMEM((parts, tokens, width // parts), bf16),
            sems((11,)),
            sems((sends,)),
            sems((inner, outer)),
            sems((sends,)),
            sems((inner, outer)),
            sems((sends,)),
            sems((inner, outer)),
            sems((parts,)),
            sems((parts,)),
        ],
        compiler_params=pltpu.CompilerParams(collective_id=0, has_side_effects=True),
        name="joint_attention",
    )(
        queries, keys, values, text_keys, text_values, conv_weight, out_weight, image_hidden,
        gate, jnp.asarray(row_table), jnp.asarray(col_table),
    )


def solution(mesh):
    placed = (
        P(("groups", "seq"), "tensor"),
        P(("groups", "seq"), "tensor"),
        P(("groups", "seq"), "tensor"),
        P(("groups", "seq"), "tensor"),
        P(("groups", "seq"), "tensor"),
        P(None, "tensor"),
        P("tensor", None),
        P(("groups", "seq"), None),
        P("groups"),
    )
    return jax.shard_map(
        functools.partial(local, mesh.shape["seq"]),
        mesh=mesh,
        in_specs=placed,
        out_specs=P(("groups", "seq"), None),
        check_vma=False,
    )
```

```python
import functools
import math

import jax
import jax.numpy as jnp
import numpy as np
from jax import lax
from jax.experimental import pallas as pl
from jax.experimental.pallas import tpu as pltpu
from jax.sharding import PartitionSpec as P

HEAD_DIM = 128
REACH = 1
MESH = pl.DeviceIdType.MESH


def position_tables(places, row_width):
    lead = HEAD_DIM // 8
    group = HEAD_DIM * 7 // 16
    frequency = np.power(
        np.float32(10000.0), -(2.0 * np.arange(group // 2, dtype=np.float32)) / np.float32(group)
    ).astype(np.float32)
    pair_frequency = np.repeat(frequency, 2)
    sign = np.where(np.arange(group) % 2 == 0, -1.0, 1.0)

    def turned(positions):
        angles = (np.asarray(positions, np.float32)[:, None] * pair_frequency[None, :]).astype(np.float64)
        return np.cos(angles), np.sin(angles) * sign

    def row_part(positions):
        cos_part, sin_part = turned(positions)
        count = len(positions)
        full_cos = np.zeros((count, HEAD_DIM))
        full_sin = np.zeros((count, HEAD_DIM))
        full_cos[:, :lead] = 1.0
        full_cos[:, lead : lead + group] = cos_part
        full_sin[:, lead : lead + group] = sin_part
        return full_cos, full_sin

    def col_part(positions):
        cos_part, sin_part = turned(positions)
        count = len(positions)
        full_cos = np.zeros((count, HEAD_DIM))
        full_sin = np.zeros((count, HEAD_DIM))
        full_cos[:, lead + group :] = cos_part
        full_sin[:, lead + group :] = sin_part
        return full_cos, full_sin

    place = np.arange(places, dtype=np.float32)
    rows = np.zeros((places, 8, HEAD_DIM))
    rows[:, 0], rows[:, 2] = row_part(2.0 * place)
    rows[:, 1], rows[:, 3] = row_part(2.0 * place + 1.0)
    rows[:, 4], rows[:, 5] = row_part(2.0 * place + 0.5)
    cos_q, sin_q = col_part(np.arange(row_width))
    cos_k, sin_k = col_part(2.0 * np.arange(row_width // 2) + 0.5)
    cols = np.concatenate([cos_q, sin_q, cos_k, sin_k], axis=0)
    return rows.astype(np.float32), cols.astype(np.float32)


def fused(
    places, inner, queries, keys, values, text_keys, text_values, conv_weight, out_weight, image_hidden,
    gate, row_table, col_table, mixed, key_buf, value_buf, text_in, text_all, query_in, key_in, value_in,
    weight_buf, hidden_buf, taps_buf, gate_buf, rows_buf, cols_buf, query_rot, attended, own_part, peer_part,
    load_sem, key_send, key_recv, value_send, value_recv, part_send, part_recv,
):
    tokens, features = query_in.shape
    heads = features // HEAD_DIM
    row_width = tokens // 2
    patches = row_width // 2
    text_rows = text_keys.shape[0]
    outer = places // inner
    parts = own_part.shape[0]
    part_width = own_part.shape[2]
    me = lax.axis_index("seq")
    core = lax.axis_index("tensor")
    along = me // inner
    across = lax.rem(me, inner)
    inner_peers = [lax.rem(across + step, inner) for step in range(1, inner)]

    def at_place(outer_at, inner_at):
        return {"seq": outer_at * inner + inner_at}

    def inside(outer_at):
        return jnp.logical_and(outer_at >= 0, outer_at < outer)

    barrier = pltpu.get_barrier_semaphore()
    near = [side * step for step in range(1, min(REACH, outer - 1) + 1) for side in (1, -1)]
    for move in near:

        @pl.when(inside(along + move))
        def _():
            pl.semaphore_signal(
                barrier, inc=1, device_id=at_place(along + move, across), device_id_type=MESH
            )

    for peer in inner_peers:
        pl.semaphore_signal(barrier, inc=1, device_id=at_place(along, peer), device_id_type=MESH)
    pl.semaphore_signal(barrier, inc=1, device_id={"tensor": 1 - core}, device_id_type=MESH)

    loads = [
        pltpu.make_async_copy(keys, key_in, load_sem.at[0]),
        pltpu.make_async_copy(conv_weight, taps_buf, load_sem.at[1]),
        pltpu.make_async_copy(row_table.at[me], rows_buf, load_sem.at[2]),
        pltpu.make_async_copy(col_table, cols_buf, load_sem.at[3]),
        pltpu.make_async_copy(values, value_in, load_sem.at[4]),
        pltpu.make_async_copy(text_keys, text_in.at[0], load_sem.at[5]),
        pltpu.make_async_copy(text_values, text_in.at[1], load_sem.at[6]),
        pltpu.make_async_copy(queries, query_in, load_sem.at[7]),
        pltpu.make_async_copy(out_weight, weight_buf, load_sem.at[8]),
        pltpu.make_async_copy(image_hidden, hidden_buf, load_sem.at[9]),
        pltpu.make_async_copy(gate, gate_buf, load_sem.at[10]),
    ]
    for load in loads:
        load.start()

    row_of = lax.broadcasted_iota(jnp.int32, (tokens, tokens), 0)
    token_of = lax.broadcasted_iota(jnp.int32, (tokens, tokens), 1)
    tap_of = row_of // patches
    wanted = (tap_of // 2) * row_width + 2 * (row_of % patches) + tap_of % 2
    pick = (token_of == wanted).astype(jnp.bfloat16)
    for load in loads[:4]:
        load.wait()
    taps = taps_buf[...].astype(jnp.float32)

    def compress(field):
        picked = jnp.dot(pick, field, preferred_element_type=jnp.float32)
        total = picked[:patches] * taps[0:1]
        for tap in range(1, 4):
            total = total + picked[tap * patches : (tap + 1) * patches] * taps[tap : tap + 1]
        return total

    my_rows = rows_buf[...]
    cos_k = my_rows[4:5] + cols_buf[2 * row_width : 2 * row_width + patches]
    sin_k = my_rows[5:6] + cols_buf[2 * row_width + patches : 2 * row_width + 2 * patches]
    even = lax.broadcasted_iota(jnp.int32, (patches, HEAD_DIM), 1) % 2 == 0
    short_raw = compress(key_in[...])
    for head in range(heads):
        lanes = slice(head * HEAD_DIM, (head + 1) * HEAD_DIM)
        raw = short_raw[:, lanes]
        swapped = jnp.where(even, pltpu.roll(raw, HEAD_DIM - 1, 1), pltpu.roll(raw, 1, 1))
        key_buf[across, along, :patches, lanes] = (raw * cos_k + swapped * sin_k).astype(jnp.bfloat16)
    loads[4].wait()
    value_buf[across, along] = compress(value_in[...]).astype(jnp.bfloat16)
    loads[5].wait()
    loads[6].wait()
    key_buf[across, along, patches:, :] = jnp.concatenate(
        [text_in[kind].astype(jnp.float32) for kind in range(2)], axis=0
    ).astype(jnp.bfloat16)

    pl.semaphore_wait(barrier, inner + sum(inside(along + move).astype(jnp.int32) for move in near))

    closing = []

    def copy_of(kind, slot, number, target):
        buf, send_sem, recv_sem = kind
        return pltpu.make_async_remote_copy(
            src_ref=buf.at[slot[0], slot[1]],
            dst_ref=buf.at[slot[0], slot[1]],
            send_sem=send_sem.at[number],
            recv_sem=recv_sem.at[slot[0], slot[1]],
            device_id=target,
            device_id_type=MESH,
        )

    def send(kind, slot, number, target, when=None):
        def begin():
            copy_of(kind, slot, number, target).start()

        def end():
            copy_of(kind, slot, number, target).wait_send()

        if when is None:
            begin()
            closing.append(end)
        else:
            pl.when(when)(begin)
            closing.append(lambda: pl.when(when)(end))

    def await_arrival(kind, slot):
        copy_of(kind, slot, 0, at_place(along, across)).wait_recv()

    carried = ((key_buf, key_send, key_recv), (value_buf, value_send, value_recv))

    def send_own():
        for kind in carried:
            for number, move in enumerate(near):
                send(kind, (across, along), number, at_place(along + move, across), inside(along + move))
            for number, peer in enumerate(inner_peers):
                send(kind, (across, along), len(near) + number, at_place(along, peer))

    def pass_on():
        first_number = len(near) + inner - 1
        for distance in range(1, outer):
            for at, kind in enumerate(carried):
                number = first_number + 2 * (distance - 1) * inner
                for side in (1, -1):
                    source = along + side * distance
                    slot = (across, jnp.clip(source, 0, outer - 1))
                    here = inside(source)
                    pl.when(here)(functools.partial(await_arrival, kind, slot))
                    if distance >= REACH:
                        further = along - side
                        send(kind, slot, number, at_place(further, across), jnp.logical_and(here, inside(further)))
                    number += 1
                    for peer in inner_peers:
                        send(kind, slot, number, at_place(along, peer), here)
                        number += 1

    def collect(kind):
        for peer in inner_peers:
            for place in range(outer):
                await_arrival(kind, (peer, place))

    send_own()

    loads[7].wait()
    first = lax.broadcasted_iota(jnp.int32, (HEAD_DIM, HEAD_DIM), 0)
    second = lax.broadcasted_iota(jnp.int32, (HEAD_DIM, HEAD_DIM), 1)
    swap = (first == second + 1 - 2 * (second % 2)).astype(jnp.bfloat16)
    col_cos = cols_buf[:row_width]
    col_sin = cols_buf[row_width : 2 * row_width]
    for row in range(2):
        cos_q = my_rows[row : row + 1] + col_cos
        sin_q = my_rows[2 + row : 3 + row] + col_sin
        rows = slice(row * row_width, (row + 1) * row_width)
        for head in range(heads):
            lanes = slice(head * HEAD_DIM, (head + 1) * HEAD_DIM)
            plain = query_in[rows, lanes]
            crossed = jnp.dot(plain, swap, preferred_element_type=jnp.float32)
            query_rot[rows, lanes] = (plain.astype(jnp.float32) * cos_q + crossed * sin_q).astype(jnp.bfloat16)

    pass_on()

    scale = 1.0 / math.sqrt(HEAD_DIM)
    transposed = (((1,), (1,)), ((), ()))
    lanes_of = [slice(head * HEAD_DIM, (head + 1) * HEAD_DIM) for head in range(heads)]

    def scores_with(keys_of):
        return [
            lax.dot_general(query_rot[:, lanes], keys_of(lanes), transposed, preferred_element_type=jnp.float32)
            for lanes in lanes_of
        ]

    def group_of(buf, at):
        return lambda lanes: buf[at, :, :patches, lanes].reshape(outer * patches, HEAD_DIM)

    scores = [scores_with(group_of(key_buf, across))]
    collect(carried[0])
    for kind in range(2):
        for place in range(places):
            start = patches + kind * text_rows
            text_all[kind, place * text_rows : (place + 1) * text_rows, :] = key_buf[
                place // outer, place % outer, start : start + text_rows
            ].astype(jnp.float32)
    scores.append(scores_with(lambda lanes: text_all[0, :, lanes].astype(jnp.bfloat16)))
    for peer in inner_peers:
        scores.append(scores_with(group_of(key_buf, peer)))

    weights, inverse = [], []
    for head in range(heads):
        top = functools.reduce(
            jnp.maximum, [jnp.max(group[head], axis=-1, keepdims=True) for group in scores]
        )
        weights.append([jnp.exp((group[head] - top) * scale).astype(jnp.bfloat16) for group in scores])
        total = sum(jnp.sum(group.astype(jnp.float32), axis=-1, keepdims=True) for group in weights[head])
        inverse.append(1.0 / total)
    summed = [
        jnp.dot(weights[head][0], group_of(value_buf, across)(lanes), preferred_element_type=jnp.float32)
        + jnp.dot(
            weights[head][1], text_all[1, :, lanes].astype(jnp.bfloat16), preferred_element_type=jnp.float32
        )
        for head, lanes in enumerate(lanes_of)
    ]
    loads[8].wait()
    loads[9].wait()
    loads[10].wait()

    collect(carried[1])
    for head, lanes in enumerate(lanes_of):
        for number, peer in enumerate(inner_peers):
            summed[head] = summed[head] + jnp.dot(
                weights[head][2 + number], group_of(value_buf, peer)(lanes), preferred_element_type=jnp.float32
            )
        attended[:, lanes] = (summed[head] * inverse[head]).astype(jnp.bfloat16)

    exchanges = []
    for part in range(parts):
        lanes = slice(part * part_width, (part + 1) * part_width)
        own_part[part] = jnp.dot(
            attended[...], weight_buf[:, lanes], preferred_element_type=jnp.float32
        ).astype(jnp.bfloat16)
        exchange = pltpu.make_async_remote_copy(
            src_ref=own_part.at[part],
            dst_ref=peer_part.at[part],
            send_sem=part_send.at[part],
            recv_sem=part_recv.at[part],
            device_id={"tensor": 1 - core},
            device_id_type=MESH,
        )
        exchange.start()
        exchanges.append(exchange)
    for end in closing:
        end()
    gates = gate_buf[...].astype(jnp.float32).reshape(1, parts * part_width)
    for part in range(parts):
        lanes = slice(part * part_width, (part + 1) * part_width)
        exchanges[part].wait_recv()
        projected = own_part[part].astype(jnp.float32) + peer_part[part].astype(jnp.float32)
        mixed[:, lanes] = (
            hidden_buf[:, lanes].astype(jnp.float32) + gates[:, lanes] * projected
        ).astype(jnp.bfloat16)
    for exchange in exchanges:
        exchange.wait_send()


def local(
    places, queries, keys, values, text_keys, text_values, conv_weight, out_weight, image_hidden, gate
):
    tokens, features = queries.shape
    width = out_weight.shape[1]
    patches = tokens // 4
    text_rows = text_keys.shape[0]
    inner = 1 << ((places.bit_length() - 1) // 2)
    if places % inner:
        inner = 1
    row_table, col_table = position_tables(places, tokens // 2)
    parts = 3
    bf16, f32 = jnp.bfloat16, jnp.float32
    hbm = pl.BlockSpec(memory_space=pl.ANY)
    vmem = pl.BlockSpec(memory_space=pltpu.VMEM)
    sems = pltpu.SemaphoreType.DMA
    outer = places // inner
    sends = 2 * REACH + inner - 1 + 2 * (outer - 1) * inner
    return pl.pallas_call(
        functools.partial(fused, places, inner),
        out_shape=pltpu.VMEM((tokens, width), bf16),
        in_specs=[hbm] * 11,
        out_specs=vmem,
        scratch_shapes=[
            pltpu.VMEM((inner, outer, patches + 2 * text_rows, features), bf16),
            pltpu.VMEM((inner, outer, patches, features), bf16),
            pltpu.VMEM((2, text_rows, features), bf16),
            pltpu.VMEM((2, places * text_rows, features), f32),
            pltpu.VMEM((tokens, features), bf16),
            pltpu.VMEM((tokens, features), bf16),
            pltpu.VMEM((tokens, features), bf16),
            pltpu.VMEM((features, width), bf16),
            pltpu.VMEM((tokens, width), bf16),
            pltpu.VMEM(conv_weight.shape, bf16),
            pltpu.VMEM(gate.shape, bf16),
            pltpu.VMEM(row_table.shape[1:], f32),
            pltpu.VMEM(col_table.shape, f32),
            pltpu.VMEM((tokens, features), bf16),
            pltpu.VMEM((tokens, features), bf16),
            pltpu.VMEM((parts, tokens, width // parts), bf16),
            pltpu.VMEM((parts, tokens, width // parts), bf16),
            sems((11,)),
            sems((sends,)),
            sems((inner, outer)),
            sems((sends,)),
            sems((inner, outer)),
            sems((parts,)),
            sems((parts,)),
        ],
        compiler_params=pltpu.CompilerParams(collective_id=0, has_side_effects=True),
        name="joint_attention",
    )(
        queries, keys, values, text_keys, text_values, conv_weight, out_weight, image_hidden,
        gate, jnp.asarray(row_table), jnp.asarray(col_table),
    )


def solution(mesh):
    placed = (
        P(("groups", "seq"), "tensor"),
        P(("groups", "seq"), "tensor"),
        P(("groups", "seq"), "tensor"),
        P(("groups", "seq"), "tensor"),
        P(("groups", "seq"), "tensor"),
        P(None, "tensor"),
        P("tensor", None),
        P(("groups", "seq"), None),
        P("groups"),
    )
    return jax.shard_map(
        functools.partial(local, mesh.shape["seq"]),
        mesh=mesh,
        in_specs=placed,
        out_specs=P(("groups", "seq"), None),
        check_vma=False,
    )
```

```python
import functools
import math

import jax
import jax.numpy as jnp
import numpy as np
from jax import lax
from jax.experimental import pallas as pl
from jax.experimental.pallas import tpu as pltpu
from jax.sharding import PartitionSpec as P

HEAD_DIM = 128
REACH = 1
PIECES = 2
MESH = pl.DeviceIdType.MESH


def position_tables(places, row_width):
    lead = HEAD_DIM // 8
    group = HEAD_DIM * 7 // 16
    frequency = np.power(
        np.float32(10000.0), -(2.0 * np.arange(group // 2, dtype=np.float32)) / np.float32(group)
    ).astype(np.float32)
    pair_frequency = np.repeat(frequency, 2)
    sign = np.where(np.arange(group) % 2 == 0, -1.0, 1.0)

    def turned(positions):
        angles = (np.asarray(positions, np.float32)[:, None] * pair_frequency[None, :]).astype(np.float64)
        return np.cos(angles), np.sin(angles) * sign

    def row_part(positions):
        cos_part, sin_part = turned(positions)
        count = len(positions)
        full_cos = np.zeros((count, HEAD_DIM))
        full_sin = np.zeros((count, HEAD_DIM))
        full_cos[:, :lead] = 1.0
        full_cos[:, lead : lead + group] = cos_part
        full_sin[:, lead : lead + group] = sin_part
        return full_cos, full_sin

    def col_part(positions):
        cos_part, sin_part = turned(positions)
        count = len(positions)
        full_cos = np.zeros((count, HEAD_DIM))
        full_sin = np.zeros((count, HEAD_DIM))
        full_cos[:, lead + group :] = cos_part
        full_sin[:, lead + group :] = sin_part
        return full_cos, full_sin

    place = np.arange(places, dtype=np.float32)
    rows = np.zeros((places, 8, HEAD_DIM))
    rows[:, 0], rows[:, 2] = row_part(2.0 * place)
    rows[:, 1], rows[:, 3] = row_part(2.0 * place + 1.0)
    rows[:, 4], rows[:, 5] = row_part(2.0 * place + 0.5)
    cos_q, sin_q = col_part(np.arange(row_width))
    cos_k, sin_k = col_part(2.0 * np.arange(row_width // 2) + 0.5)
    cols = np.concatenate([cos_q, sin_q, cos_k, sin_k], axis=0)
    return rows.astype(np.float32), cols.astype(np.float32)


def fused(
    places, inner, queries, keys, values, text_keys, text_values, conv_weight, out_weight, image_hidden,
    gate, row_table, col_table, mixed, key_buf, value_buf, text_in, text_all, query_in, key_in, value_in,
    weight_buf, hidden_buf, taps_buf, gate_buf, rows_buf, cols_buf, query_rot, attended, own_part, peer_part,
    load_sem, key_send, key_recv, value_send, value_recv, part_send, part_recv,
):
    tokens, features = query_in.shape
    heads = features // HEAD_DIM
    row_width = tokens // 2
    patches = row_width // 2
    text_rows = text_keys.shape[0]
    outer = places // inner
    parts = own_part.shape[0]
    part_width = own_part.shape[2]
    me = lax.axis_index("seq")
    core = lax.axis_index("tensor")
    along = me // inner
    across = lax.rem(me, inner)
    inner_peers = [lax.rem(across + step, inner) for step in range(1, inner)]

    def at_place(outer_at, inner_at):
        return {"seq": outer_at * inner + inner_at}

    def inside(outer_at):
        return jnp.logical_and(outer_at >= 0, outer_at < outer)

    barrier = pltpu.get_barrier_semaphore()
    near = [side * step for step in range(1, min(REACH, outer - 1) + 1) for side in (1, -1)]
    for move in near:

        @pl.when(inside(along + move))
        def _():
            pl.semaphore_signal(
                barrier, inc=1, device_id=at_place(along + move, across), device_id_type=MESH
            )

    for peer in inner_peers:
        pl.semaphore_signal(barrier, inc=1, device_id=at_place(along, peer), device_id_type=MESH)
    pl.semaphore_signal(barrier, inc=1, device_id={"tensor": 1 - core}, device_id_type=MESH)

    loads = [
        pltpu.make_async_copy(keys, key_in, load_sem.at[0]),
        pltpu.make_async_copy(conv_weight, taps_buf, load_sem.at[1]),
        pltpu.make_async_copy(row_table.at[me], rows_buf, load_sem.at[2]),
        pltpu.make_async_copy(col_table, cols_buf, load_sem.at[3]),
        pltpu.make_async_copy(values, value_in, load_sem.at[4]),
        pltpu.make_async_copy(text_keys, text_in.at[0], load_sem.at[5]),
        pltpu.make_async_copy(text_values, text_in.at[1], load_sem.at[6]),
        pltpu.make_async_copy(queries, query_in, load_sem.at[7]),
        pltpu.make_async_copy(out_weight, weight_buf, load_sem.at[8]),
        pltpu.make_async_copy(image_hidden, hidden_buf, load_sem.at[9]),
        pltpu.make_async_copy(gate, gate_buf, load_sem.at[10]),
    ]
    for load in loads:
        load.start()

    row_of = lax.broadcasted_iota(jnp.int32, (tokens, tokens), 0)
    token_of = lax.broadcasted_iota(jnp.int32, (tokens, tokens), 1)
    tap_of = row_of // patches
    wanted = (tap_of // 2) * row_width + 2 * (row_of % patches) + tap_of % 2
    pick = (token_of == wanted).astype(jnp.bfloat16)
    for load in loads[:4]:
        load.wait()
    taps = taps_buf[...].astype(jnp.float32)

    def compress(field):
        picked = jnp.dot(pick, field, preferred_element_type=jnp.float32)
        total = picked[:patches] * taps[0:1]
        for tap in range(1, 4):
            total = total + picked[tap * patches : (tap + 1) * patches] * taps[tap : tap + 1]
        return total

    my_rows = rows_buf[...]
    cos_k = my_rows[4:5] + cols_buf[2 * row_width : 2 * row_width + patches]
    sin_k = my_rows[5:6] + cols_buf[2 * row_width + patches : 2 * row_width + 2 * patches]
    even = lax.broadcasted_iota(jnp.int32, (patches, HEAD_DIM), 1) % 2 == 0
    short_raw = compress(key_in[...])
    for head in range(heads):
        lanes = slice(head * HEAD_DIM, (head + 1) * HEAD_DIM)
        raw = short_raw[:, lanes]
        swapped = jnp.where(even, pltpu.roll(raw, HEAD_DIM - 1, 1), pltpu.roll(raw, 1, 1))
        key_buf[across, along, :patches, lanes] = (raw * cos_k + swapped * sin_k).astype(jnp.bfloat16)
    loads[4].wait()
    value_buf[across, along] = compress(value_in[...]).astype(jnp.bfloat16)
    loads[5].wait()
    loads[6].wait()
    key_buf[across, along, patches:, :] = jnp.concatenate(
        [text_in[kind].astype(jnp.float32) for kind in range(2)], axis=0
    ).astype(jnp.bfloat16)

    pl.semaphore_wait(barrier, inner + sum(inside(along + move).astype(jnp.int32) for move in near))

    closing = []

    def copy_of(kind, slot, number, target):
        buf, send_sem, recv_sem = kind
        return pltpu.make_async_remote_copy(
            src_ref=buf.at[slot[0], slot[1]],
            dst_ref=buf.at[slot[0], slot[1]],
            send_sem=send_sem.at[number],
            recv_sem=recv_sem.at[slot[0], slot[1]],
            device_id=target,
            device_id_type=MESH,
        )

    def send(kind, slot, number, target, when=None):
        def begin():
            copy_of(kind, slot, number, target).start()

        def end():
            copy_of(kind, slot, number, target).wait_send()

        if when is None:
            begin()
            closing.append(end)
        else:
            pl.when(when)(begin)
            closing.append(lambda: pl.when(when)(end))

    def await_arrival(kind, slot):
        copy_of(kind, slot, 0, at_place(along, across)).wait_recv()

    pieces = key_send.shape[0]
    width = features // pieces
    carried = [
        (buf.at[:, :, :, piece * width : (piece + 1) * width], send_sem.at[piece], recv_sem.at[piece])
        for buf, send_sem, recv_sem in ((key_buf, key_send, key_recv), (value_buf, value_send, value_recv))
        for piece in range(pieces)
    ]

    def send_own():
        for kind in carried:
            for number, move in enumerate(near):
                send(kind, (across, along), number, at_place(along + move, across), inside(along + move))
            for number, peer in enumerate(inner_peers):
                send(kind, (across, along), len(near) + number, at_place(along, peer))

    def pass_on():
        first_number = len(near) + inner - 1
        for distance in range(1, outer):
            for at, kind in enumerate(carried):
                number = first_number + 2 * (distance - 1) * inner
                for side in (1, -1):
                    source = along + side * distance
                    slot = (across, jnp.clip(source, 0, outer - 1))
                    here = inside(source)
                    pl.when(here)(functools.partial(await_arrival, kind, slot))
                    if distance >= REACH:
                        further = along - side
                        send(kind, slot, number, at_place(further, across), jnp.logical_and(here, inside(further)))
                    number += 1
                    for peer in inner_peers:
                        send(kind, slot, number, at_place(along, peer), here)
                        number += 1

    def collect(kind):
        for peer in inner_peers:
            for place in range(outer):
                await_arrival(kind, (peer, place))

    send_own()

    loads[7].wait()
    first = lax.broadcasted_iota(jnp.int32, (HEAD_DIM, HEAD_DIM), 0)
    second = lax.broadcasted_iota(jnp.int32, (HEAD_DIM, HEAD_DIM), 1)
    swap = (first == second + 1 - 2 * (second % 2)).astype(jnp.bfloat16)
    col_cos = cols_buf[:row_width]
    col_sin = cols_buf[row_width : 2 * row_width]
    for row in range(2):
        cos_q = my_rows[row : row + 1] + col_cos
        sin_q = my_rows[2 + row : 3 + row] + col_sin
        rows = slice(row * row_width, (row + 1) * row_width)
        for head in range(heads):
            lanes = slice(head * HEAD_DIM, (head + 1) * HEAD_DIM)
            plain = query_in[rows, lanes]
            crossed = jnp.dot(plain, swap, preferred_element_type=jnp.float32)
            query_rot[rows, lanes] = (plain.astype(jnp.float32) * cos_q + crossed * sin_q).astype(jnp.bfloat16)

    pass_on()

    scale = 1.0 / math.sqrt(HEAD_DIM)
    transposed = (((1,), (1,)), ((), ()))
    lanes_of = [slice(head * HEAD_DIM, (head + 1) * HEAD_DIM) for head in range(heads)]

    def scores_with(keys_of):
        return [
            lax.dot_general(query_rot[:, lanes], keys_of(lanes), transposed, preferred_element_type=jnp.float32)
            for lanes in lanes_of
        ]

    def group_of(buf, at):
        return lambda lanes: buf[at, :, :patches, lanes].reshape(outer * patches, HEAD_DIM)

    scores = [scores_with(group_of(key_buf, across))]
    for kind in carried[:pieces]:
        collect(kind)
    for kind in range(2):
        for place in range(places):
            start = patches + kind * text_rows
            text_all[kind, place * text_rows : (place + 1) * text_rows, :] = key_buf[
                place // outer, place % outer, start : start + text_rows
            ].astype(jnp.float32)
    scores.append(scores_with(lambda lanes: text_all[0, :, lanes].astype(jnp.bfloat16)))
    for peer in inner_peers:
        scores.append(scores_with(group_of(key_buf, peer)))

    weights, inverse = [], []
    for head in range(heads):
        top = functools.reduce(
            jnp.maximum, [jnp.max(group[head], axis=-1, keepdims=True) for group in scores]
        )
        weights.append([jnp.exp((group[head] - top) * scale).astype(jnp.bfloat16) for group in scores])
        total = sum(jnp.sum(group.astype(jnp.float32), axis=-1, keepdims=True) for group in weights[head])
        inverse.append(1.0 / total)
    summed = [
        jnp.dot(weights[head][0], group_of(value_buf, across)(lanes), preferred_element_type=jnp.float32)
        + jnp.dot(
            weights[head][1], text_all[1, :, lanes].astype(jnp.bfloat16), preferred_element_type=jnp.float32
        )
        for head, lanes in enumerate(lanes_of)
    ]
    loads[8].wait()
    loads[9].wait()
    loads[10].wait()

    for kind in carried[pieces:]:
        collect(kind)
    for head, lanes in enumerate(lanes_of):
        for number, peer in enumerate(inner_peers):
            summed[head] = summed[head] + jnp.dot(
                weights[head][2 + number], group_of(value_buf, peer)(lanes), preferred_element_type=jnp.float32
            )
        attended[:, lanes] = (summed[head] * inverse[head]).astype(jnp.bfloat16)

    exchanges = []
    for part in range(parts):
        lanes = slice(part * part_width, (part + 1) * part_width)
        own_part[part] = jnp.dot(
            attended[...], weight_buf[:, lanes], preferred_element_type=jnp.float32
        ).astype(jnp.bfloat16)
        exchange = pltpu.make_async_remote_copy(
            src_ref=own_part.at[part],
            dst_ref=peer_part.at[part],
            send_sem=part_send.at[part],
            recv_sem=part_recv.at[part],
            device_id={"tensor": 1 - core},
            device_id_type=MESH,
        )
        exchange.start()
        exchanges.append(exchange)
    for end in closing:
        end()
    gates = gate_buf[...].astype(jnp.float32).reshape(1, parts * part_width)
    for part in range(parts):
        lanes = slice(part * part_width, (part + 1) * part_width)
        exchanges[part].wait_recv()
        projected = own_part[part].astype(jnp.float32) + peer_part[part].astype(jnp.float32)
        mixed[:, lanes] = (
            hidden_buf[:, lanes].astype(jnp.float32) + gates[:, lanes] * projected
        ).astype(jnp.bfloat16)
    for exchange in exchanges:
        exchange.wait_send()


def local(
    places, queries, keys, values, text_keys, text_values, conv_weight, out_weight, image_hidden, gate
):
    tokens, features = queries.shape
    width = out_weight.shape[1]
    patches = tokens // 4
    text_rows = text_keys.shape[0]
    inner = 1 << ((places.bit_length() - 1) // 2)
    if places % inner:
        inner = 1
    row_table, col_table = position_tables(places, tokens // 2)
    parts = 3
    bf16, f32 = jnp.bfloat16, jnp.float32
    hbm = pl.BlockSpec(memory_space=pl.ANY)
    vmem = pl.BlockSpec(memory_space=pltpu.VMEM)
    sems = pltpu.SemaphoreType.DMA
    outer = places // inner
    sends = 2 * REACH + inner - 1 + 2 * (outer - 1) * inner
    return pl.pallas_call(
        functools.partial(fused, places, inner),
        out_shape=pltpu.VMEM((tokens, width), bf16),
        in_specs=[hbm] * 11,
        out_specs=vmem,
        scratch_shapes=[
            pltpu.VMEM((inner, outer, patches + 2 * text_rows, features), bf16),
            pltpu.VMEM((inner, outer, patches, features), bf16),
            pltpu.VMEM((2, text_rows, features), bf16),
            pltpu.VMEM((2, places * text_rows, features), f32),
            pltpu.VMEM((tokens, features), bf16),
            pltpu.VMEM((tokens, features), bf16),
            pltpu.VMEM((tokens, features), bf16),
            pltpu.VMEM((features, width), bf16),
            pltpu.VMEM((tokens, width), bf16),
            pltpu.VMEM(conv_weight.shape, bf16),
            pltpu.VMEM(gate.shape, bf16),
            pltpu.VMEM(row_table.shape[1:], f32),
            pltpu.VMEM(col_table.shape, f32),
            pltpu.VMEM((tokens, features), bf16),
            pltpu.VMEM((tokens, features), bf16),
            pltpu.VMEM((parts, tokens, width // parts), bf16),
            pltpu.VMEM((parts, tokens, width // parts), bf16),
            sems((11,)),
            sems((PIECES, sends)),
            sems((PIECES, inner, outer)),
            sems((PIECES, sends)),
            sems((PIECES, inner, outer)),
            sems((parts,)),
            sems((parts,)),
        ],
        compiler_params=pltpu.CompilerParams(collective_id=0, has_side_effects=True),
        name="joint_attention",
    )(
        queries, keys, values, text_keys, text_values, conv_weight, out_weight, image_hidden,
        gate, jnp.asarray(row_table), jnp.asarray(col_table),
    )


def solution(mesh):
    placed = (
        P(("groups", "seq"), "tensor"),
        P(("groups", "seq"), "tensor"),
        P(("groups", "seq"), "tensor"),
        P(("groups", "seq"), "tensor"),
        P(("groups", "seq"), "tensor"),
        P(None, "tensor"),
        P("tensor", None),
        P(("groups", "seq"), None),
        P("groups"),
    )
    return jax.shard_map(
        functools.partial(local, mesh.shape["seq"]),
        mesh=mesh,
        in_specs=placed,
        out_specs=P(("groups", "seq"), None),
        check_vma=False,
    )
```
